32 devices in a mesh: row: 4 (over z), col: 8 (over y, x, core).
Axes of the slice: x: 2, y: 2, z: 4, core: 2. Of those that a mesh axis runs over, the one named last changes fastest.
Arguments:
- integrals: bfloat16 [5120, 5120], P('row', 'col'), may hold values from -6 to 6
- amplitudes: bfloat16 [5120, 4096], P('row', 'col'), may hold values from -0.078125 to 0.078125
- int_shape: int32 [20, 20], P('row'), may hold values 0 or 1
- amp_shape: int32 [20, 16], P(None, 'col'), may hold values 0 or 1
Outputs:
- ladder: bfloat16 [5120, 4096], P('row', 'col')
The draws below stay inside these ranges and needn't reach their ends.
All inputs are finite; a program needn't handle non-finite values. No bound on the sum of `int_shape` or of `amp_shape` on one device may be relied on, other than what follows from the above.
Results may differ from the reference program's by a relative error of at most 0.001.
Values may be sent and summed in bfloat16 or wider, within the bound.
A program may use at most 192 MiB of HBM per device.

```python
import jax
import jax.numpy as jnp
from jax import lax

TILE = 256
ROW_TILES_DEV = 5
ROW_TILES = 20
K_TILES = 20
COL_TILES = 16
VROWS = 5120
OCOLS = 4096
KSUM = 5120
N_ROW = 4


def touch_ends(array, stream_key, smallest, largest):
    shape = array.shape
    spot = [jax.random.randint(jax.random.fold_in(stream_key, axis), (), 0, shape[axis]) for axis in range(len(shape))]
    array = array.at[tuple(spot)].set(smallest)
    longest = shape.index(max(shape))
    spot[longest] = (spot[longest] + 1) % shape[longest]
    return array.at[tuple(spot)].set(largest)


def levels(own_key, shape, shards, least, largest):
    level = 1.0
    for dim, shards_of in shards:
        steps = jax.random.uniform(jax.random.fold_in(jax.random.fold_in(own_key, 6), dim), (shards_of,), jnp.float32, least / len(shards), largest / len(shards))
        level = level * jnp.repeat(jnp.exp(steps), shape[dim] // shards_of).reshape((-1,) + (1,) * (len(shape) - 1 - dim))
    return level


def scatter_about(own_key, extent, width, reach, shards=(), kind=jnp.bfloat16):
    factor_of = levels(own_key, extent, shards, -0.22, 0.18) if shards else 1.0
    array = jax.random.normal(own_key, extent, jnp.float32) * width * factor_of
    return jnp.minimum(jnp.maximum(array, -reach), reach).astype(kind)


def setup_inputs(seed: int = 0) -> dict:
    key_list = jax.random.split(jax.random.key(seed), 5)
    integrals = scatter_about(key_list[0], (VROWS, KSUM), 1.0, 6.0, ((0, 4), (1, 8)))
    amplitudes = scatter_about(key_list[1], (KSUM, OCOLS), KSUM ** -0.5, 0.078125, ((0, 4), (1, 8)))
    int_shape = touch_ends((jax.random.randint(key_list[2], (ROW_TILES, K_TILES), 0, 3) < 2).astype(jnp.int32), jax.random.fold_in(key_list[2], 1), 0, 1)
    amp_shape = touch_ends((jax.random.randint(key_list[3], (K_TILES, COL_TILES), 0, 3) < 2).astype(jnp.int32), jax.random.fold_in(key_list[3], 1), 0, 1)
    return {"integrals": integrals, "amplitudes": amplitudes, "int_shape": int_shape, "amp_shape": amp_shape}


def expand_shape(shape_mask):
    return jnp.repeat(jnp.repeat(shape_mask, TILE, axis=0), TILE, axis=1).astype(jnp.bfloat16)


def reference(integrals, amplitudes, int_shape, amp_shape):
    masked_amp = amplitudes * expand_shape(amp_shape)
    row_blocks = integrals.reshape(N_ROW, ROW_TILES_DEV * TILE, K_TILES * TILE)
    shape_blocks = int_shape.reshape(N_ROW, ROW_TILES_DEV, K_TILES)

    def one_block(pair):
        block, shape_block = pair
        masked_int = block * expand_shape(shape_block)
        return jnp.dot(masked_int, masked_amp, preferred_element_type=jnp.float32).astype(jnp.bfloat16)

    ladder = lax.map(one_block, (row_blocks, shape_blocks))
    return ladder.reshape(N_ROW * ROW_TILES_DEV * TILE, masked_amp.shape[1])
```

```python
import functools

import jax
import jax.numpy as jnp
from jax import lax
from jax.experimental import pallas as pl
from jax.experimental.pallas import tpu as pltpu
from jax.sharding import PartitionSpec as P

TILE = 256
CORES = 2
MESH = pl.DeviceIdType.MESH


class Plan:
    def __init__(self, n_row, n_col, rows, i_cols, a_rows, a_cols):
        self.R, self.C = n_row, n_col
        self.G = n_col // CORES
        self.nb = self.G.bit_length() - 1
        assert self.G == 1 << self.nb and self.G == n_row
        assert a_rows == i_cols * CORES and a_rows % TILE == 0 and rows % TILE == 0
        self.rows, self.i_cols, self.a_rows, self.a_cols = rows, i_cols, a_rows, a_cols
        self.RT, self.KT, self.QT = rows // TILE, a_rows // TILE, a_cols // TILE
        self.piece = {r: (r * self.nb) // self.RT for r in range(self.RT)}

    def dim(self, r, t):
        return (self.piece[r] + t) % self.nb

    def known(self, r, t):
        masks = [0]
        for u in range(t):
            masks += [m ^ (1 << self.dim(r, u)) for m in masks]
        return masks

    def sends(self, d):
        items = []
        for r in range(self.RT):
            for t in range(self.nb):
                if self.dim(r, t) == d:
                    items += [(t, m, r) for m in self.known(r, t)]
        return sorted(items, key=lambda i: (i[0], bin(i[1]).count("1"), i[2]))

    def events(self):
        out = []
        for d in range(self.nb):
            for n, (t, m, r) in enumerate(self.sends(d)):
                out.append(((n + 1) * self.i_cols, ("i", t, m ^ (1 << d), r)))
        for n in range((self.R - 1) * self.KT):
            out.append(((n + 1) * self.a_cols, ("a", 1 + n // self.KT, n % self.KT)))
        return [e for _, e in sorted(out, key=lambda e: e[0])]


def kernel(plan, imask, amask, i_hbm, a_hbm, o_ref, i_all, a_all, acc,
           local_sem, i_send, i_sib, i_recv, a_send, a_recv):
    p = plan
    z, c = lax.axis_index("row"), lax.axis_index("col")
    g, core = c // CORES, lax.rem(c, CORES)
    sibling = (z, g * CORES + 1 - core)

    def flip(value, mask):
        for b in range(p.nb):
            if mask >> b & 1:
                value = value + (1 << b) - (2 << b) * lax.rem(value // (1 << b), 2)
        return value

    def partner(d):
        return (z, flip(g, 1 << d) * CORES + core)

    has = {1: z < p.R - 1, -1: z > 0}

    bar = pltpu.get_barrier_semaphore()
    pl.semaphore_signal(bar, inc=1, device_id=sibling, device_id_type=MESH)
    for d in range(p.nb):
        pl.semaphore_signal(bar, inc=1, device_id=partner(d), device_id_type=MESH)
    for s in (1, -1):
        @pl.when(has[s])
        def _():
            pl.semaphore_signal(bar, inc=1, device_id=(z + s, c), device_id_type=MESH)
    ends = (z + p.R - 1) // p.R + (2 * p.R - 2 - z) // p.R
    pl.semaphore_wait(bar, 1 + p.nb + ends)

    def i_place(m, r, which):
        lanes = pl.ds(pl.multiple_of(which * p.i_cols, 128), p.i_cols)
        return i_all.at[flip(g, m), pl.ds(r * TILE, TILE), lanes]

    def i_source(m, r):
        return i_hbm.at[pl.ds(r * TILE, TILE)] if m == 0 else i_place(m, r, core)

    def i_link(d, m, r):
        return pltpu.make_async_remote_copy(
            i_source(m, r), i_place(m, r, core), i_send.at[d, m, r],
            i_recv.at[flip(g, m), core, r], device_id=partner(d), device_id_type=MESH)

    def i_cross(m, r):
        return pltpu.make_async_remote_copy(
            i_source(m, r), i_place(m, r, core), i_sib.at[m, r],
            i_recv.at[flip(g, m), core, r], device_id=sibling, device_id_type=MESH)

    def i_wait(m, r, which):
        pltpu.make_async_remote_copy(
            i_place(m, r, which), i_place(m, r, which), i_sib.at[m, r],
            i_recv.at[flip(g, m), which, r], device_id=sibling, device_id_type=MESH).wait_recv()

    def a_place(t, kt, s):
        return a_all.at[z - s * t, pl.ds(kt * TILE, TILE)]

    def a_link(t, kt, s):
        src = a_hbm.at[pl.ds(kt * TILE, TILE)] if t == 0 else a_place(t, kt, s)
        return pltpu.make_async_remote_copy(
            src, a_place(t, kt, s), a_send.at[(1 - s) // 2, t, kt],
            a_recv.at[z - s * t, kt], device_id=(z + s, c), device_id_type=MESH)

    def origin_ok(t, s):
        return z >= t if s == 1 else z + t <= p.R - 1

    for kt in range(p.KT):
        for s in (1, -1):
            @pl.when(has[s])
            def _():
                a_link(0, kt, s).start()
    own = [[(m, r) for _, m, r in p.sends(d) if m == 0] for d in range(p.nb)]
    for n in range(p.RT):
        for d in range(p.nb):
            i_link(d, *own[d][n]).start()
    for r in range(p.RT):
        i_cross(0, r).start()
    lanes = pl.ds(pl.multiple_of(core * p.i_cols, 128), p.i_cols)
    own_i = pltpu.make_async_copy(i_hbm, i_all.at[g, :, lanes], local_sem.at[0])
    own_a = pltpu.make_async_copy(a_hbm, a_all.at[z], local_sem.at[1])
    own_i.start()
    own_a.start()
    acc[...] = jnp.zeros_like(acc)

    def multiply(j, kt):
        k = j * p.KT + kt

        @pl.loop(0, p.RT)
        def _(r):
            at = pl.ds(pl.multiple_of(r * TILE, TILE), TILE)
            left = i_all[j, at, pl.ds(kt * TILE, TILE)]
            for q in range(p.QT):
                cols = pl.ds(q * TILE, TILE)
                part = jnp.dot(left, a_all[j, pl.ds(kt * TILE, TILE), cols],
                               preferred_element_type=jnp.float32)
                keep = (imask[r, k] * amask[k, q]).astype(jnp.float32)
                acc[at, cols] += keep * part

    def a_arrive(t, kt):
        for s in (1, -1):
            @pl.when(origin_ok(t, s))
            def _():
                pltpu.make_async_remote_copy(
                    a_place(t, kt, s), a_place(t, kt, s), a_send.at[0, 0, kt],
                    a_recv.at[z - s * t, kt], device_id=sibling, device_id_type=MESH).wait_recv()

                @pl.when(has[s])
                def _():
                    a_link(t, kt, s).start()

    def a_use(t, kt):
        for s in (1, -1):
            @pl.when(origin_ok(t, s))
            def _():
                multiply(z - s * t, kt)

    events = p.events()
    last_i = max(n for n, e in enumerate(events) if e[0] == "i")
    pending = []
    for n, event in enumerate(events):
        if event[0] == "a":
            _, t, kt = event
            a_arrive(t, kt)
            if n < last_i:
                pending.append((t, kt))
            else:
                a_use(t, kt)
            continue
        _, t, m, r = event
        i_wait(m, r, core)
        for u in range(t + 1, p.nb):
            i_link(p.dim(r, u), m, r).start()
        i_cross(m, r).start()
        if n == last_i:
            own_i.wait()
            own_a.wait()
            for m in range(p.G):
                for r in range(p.RT):
                    i_wait(m, r, 1 - core)
            for kt in range(p.KT):
                multiply(z, kt)
            for item in pending:
                a_use(*item)
    o_ref[...] = acc[...].astype(o_ref.dtype)

    for d in range(p.nb):
        for _, m, r in p.sends(d):
            i_link(d, m, r).wait_send()
    for m in range(p.G):
        for r in range(p.RT):
            i_cross(m, r).wait_send()
    for t in range(p.R - 1):
        for kt in range(p.KT):
            for s in (1, -1):
                @pl.when(has[s] & origin_ok(t, s))
                def _():
                    a_link(t, kt, s).wait_send()


def per_device(n_row, n_col, integrals, amplitudes, int_shape, amp_shape):
    rows, i_cols = integrals.shape
    a_rows, a_cols = amplitudes.shape
    p = Plan(n_row, n_col, rows, i_cols, a_rows, a_cols)
    dma = pltpu.SemaphoreType.DMA
    return pl.pallas_call(
        functools.partial(kernel, p),
        out_shape=jax.ShapeDtypeStruct((rows, a_cols), jnp.bfloat16),
        in_specs=[pl.BlockSpec(memory_space=pltpu.SMEM)] * 2 + [pl.BlockSpec(memory_space=pl.ANY)] * 2,
        out_specs=pl.BlockSpec(memory_space=pltpu.VMEM),
        scratch_shapes=[
            pltpu.VMEM((p.G, rows, i_cols * CORES), jnp.bfloat16),
            pltpu.VMEM((p.R, a_rows, a_cols), jnp.bfloat16),
            pltpu.VMEM((rows, a_cols), jnp.float32),
            dma((2,)),
            dma((p.nb, p.G, p.RT)),
            dma((p.G, p.RT)),
            dma((p.G, CORES, p.RT)),
            dma((2, p.R, p.KT)),
            dma((p.R, p.KT)),
        ],
        compiler_params=pltpu.CompilerParams(
            collective_id=0, has_side_effects=True, vmem_limit_bytes=60 * 2**20
        ),
    )(int_shape, amp_shape, integrals, amplitudes)


def solution(mesh):
    in_specs = (P("row", "col"), P("row", "col"), P("row", None), P(None, "col"))
    out_specs = P("row", "col")
    body = functools.partial(per_device, mesh.shape["row"], mesh.shape["col"])
    return jax.shard_map(body, mesh=mesh, in_specs=in_specs, out_specs=out_specs, check_vma=False)
```

```python
import functools

import jax
import jax.numpy as jnp
from jax import lax
from jax.experimental import pallas as pl
from jax.experimental.pallas import tpu as pltpu
from jax.sharding import PartitionSpec as P

TILE = 256
CORES = 2
MESH = pl.DeviceIdType.MESH


class Plan:
    def __init__(self, n_row, n_col, rows, i_cols, a_rows, a_cols):
        self.R, self.C = n_row, n_col
        self.G = n_col // CORES
        self.nb = self.G.bit_length() - 1
        assert self.G == 1 << self.nb and self.G == n_row
        assert a_rows == i_cols * CORES and a_rows % TILE == 0 and rows % TILE == 0
        self.rows, self.i_cols, self.a_rows, self.a_cols = rows, i_cols, a_rows, a_cols
        self.RT, self.KT, self.QT = rows // TILE, a_rows // TILE, a_cols // TILE
        self.piece = {r: (r * self.nb) // self.RT for r in range(self.RT)}

    def dim(self, r, t):
        return (self.piece[r] + t) % self.nb

    def known(self, r, t):
        masks = [0]
        for u in range(t):
            masks += [m ^ (1 << self.dim(r, u)) for m in masks]
        return masks

    def sends(self, d):
        items = []
        for r in range(self.RT):
            for t in range(self.nb):
                if self.dim(r, t) == d:
                    items += [(t, m, r) for m in self.known(r, t)]
        return sorted(items, key=lambda i: (i[0], bin(i[1]).count("1"), i[2]))

    def events(self):
        out = []
        for d in range(self.nb):
            for n, (t, m, r) in enumerate(self.sends(d)):
                out.append(((n + 1) * self.i_cols, ("i", t, m ^ (1 << d), r)))
        for n in range((self.R - 1) * self.KT):
            out.append(((n + 1) * self.a_cols, ("a", 1 + n // self.KT, n % self.KT)))
        return [e for _, e in sorted(out, key=lambda e: e[0])]


def kernel(plan, imask_hbm, amask_hbm, i_hbm, a_hbm, o_ref, imask, amask, i_all, a_all, acc,
           local_sem, i_send, i_sib, i_recv, a_send, a_recv):
    p = plan
    z, c = lax.axis_index("row"), lax.axis_index("col")
    g, core = c // CORES, lax.rem(c, CORES)
    sibling = (z, g * CORES + 1 - core)

    def flip(value, mask):
        for b in range(p.nb):
            if mask >> b & 1:
                value = value + (1 << b) - (2 << b) * lax.rem(value // (1 << b), 2)
        return value

    def partner(d):
        return (z, flip(g, 1 << d) * CORES + core)

    has = {1: z < p.R - 1, -1: z > 0}

    bar = pltpu.get_barrier_semaphore()
    pl.semaphore_signal(bar, inc=1, device_id=sibling, device_id_type=MESH)
    for d in range(p.nb):
        pl.semaphore_signal(bar, inc=1, device_id=partner(d), device_id_type=MESH)
    for s in (1, -1):
        @pl.when(has[s])
        def _():
            pl.semaphore_signal(bar, inc=1, device_id=(z + s, c), device_id_type=MESH)
    ends = (z + p.R - 1) // p.R + (2 * p.R - 2 - z) // p.R
    pl.semaphore_wait(bar, 1 + p.nb + ends)

    def i_place(m, r, which):
        lanes = pl.ds(pl.multiple_of(which * p.i_cols, 128), p.i_cols)
        return i_all.at[flip(g, m), pl.ds(r * TILE, TILE), lanes]

    def i_source(m, r):
        return i_hbm.at[pl.ds(r * TILE, TILE)] if m == 0 else i_place(m, r, core)

    def i_link(d, m, r):
        return pltpu.make_async_remote_copy(
            i_source(m, r), i_place(m, r, core), i_send.at[d, m, r],
            i_recv.at[flip(g, m), core, r], device_id=partner(d), device_id_type=MESH)

    def i_cross(m, r):
        return pltpu.make_async_remote_copy(
            i_source(m, r), i_place(m, r, core), i_sib.at[m, r],
            i_recv.at[flip(g, m), core, r], device_id=sibling, device_id_type=MESH)

    def i_wait(m, r, which):
        pltpu.make_async_remote_copy(
            i_place(m, r, which), i_place(m, r, which), i_sib.at[m, r],
            i_recv.at[flip(g, m), which, r], device_id=sibling, device_id_type=MESH).wait_recv()

    def a_place(t, kt, s):
        return a_all.at[z - s * t, pl.ds(kt * TILE, TILE)]

    def a_link(t, kt, s):
        src = a_hbm.at[pl.ds(kt * TILE, TILE)] if t == 0 else a_place(t, kt, s)
        return pltpu.make_async_remote_copy(
            src, a_place(t, kt, s), a_send.at[(1 - s) // 2, t, kt],
            a_recv.at[z - s * t, kt], device_id=(z + s, c), device_id_type=MESH)

    def origin_ok(t, s):
        return z >= t if s == 1 else z + t <= p.R - 1

    for kt in range(p.KT):
        for s in (1, -1):
            @pl.when(has[s])
            def _():
                a_link(0, kt, s).start()
    own = [[(m, r) for _, m, r in p.sends(d) if m == 0] for d in range(p.nb)]
    for n in range(p.RT):
        for d in range(p.nb):
            i_link(d, *own[d][n]).start()
    for r in range(p.RT):
        i_cross(0, r).start()
    lanes = pl.ds(pl.multiple_of(core * p.i_cols, 128), p.i_cols)
    own_i = pltpu.make_async_copy(i_hbm, i_all.at[g, :, lanes], local_sem.at[0])
    own_a = pltpu.make_async_copy(a_hbm, a_all.at[z], local_sem.at[1])
    own_i.start()
    masks = [pltpu.make_async_copy(imask_hbm, imask, local_sem.at[2]),
             pltpu.make_async_copy(amask_hbm, amask, local_sem.at[3])]
    for copy in masks:
        copy.start()
    own_a.start()
    acc[...] = jnp.zeros_like(acc)

    def masked_right(j, kt):
        at = pl.ds(kt * TILE, TILE)
        k = j * p.KT + kt
        return [jnp.where(amask[q, k] != 0, a_all[j, at, pl.ds(q * TILE, TILE)], zero) for q in range(p.QT)]

    def masked_left(j, r, kt):
        at, cols = pl.ds(r * TILE, TILE), pl.ds(kt * TILE, TILE)
        return jnp.where(imask[r, j * p.KT + kt] != 0, i_all[j, at, cols], zero)

    zero = jnp.zeros((TILE, TILE), jnp.bfloat16)

    def multiply(j, kt):
        right = jnp.concatenate(masked_right(j, kt), axis=1)
        left = jnp.concatenate([masked_left(j, r, kt) for r in range(p.RT)], axis=0)
        acc[...] += jnp.dot(left, right, preferred_element_type=jnp.float32)

    def a_arrive(t, kt):
        for s in (1, -1):
            @pl.when(origin_ok(t, s))
            def _():
                pltpu.make_async_remote_copy(
                    a_place(t, kt, s), a_place(t, kt, s), a_send.at[0, 0, kt],
                    a_recv.at[z - s * t, kt], device_id=sibling, device_id_type=MESH).wait_recv()

                @pl.when(has[s])
                def _():
                    a_link(t, kt, s).start()

    def a_use(t, kt):
        for s in (1, -1):
            @pl.when(origin_ok(t, s))
            def _():
                multiply(z - s * t, kt)

    events = p.events()
    last_i = max(n for n, e in enumerate(events) if e[0] == "i")
    pending = []
    for n, event in enumerate(events):
        if event[0] == "a":
            _, t, kt = event
            a_arrive(t, kt)
            if n < last_i:
                pending.append((t, kt))
            else:
                a_use(t, kt)
            continue
        _, t, m, r = event
        i_wait(m, r, core)
        for u in range(t + 1, p.nb):
            i_link(p.dim(r, u), m, r).start()
        i_cross(m, r).start()
        if n == last_i:
            own_i.wait()
            own_a.wait()
            for copy in masks:
                copy.wait()
            for m in range(p.G):
                for r in range(p.RT):
                    i_wait(m, r, 1 - core)
            for kt in range(p.KT):
                multiply(z, kt)
            for item in pending:
                a_use(*item)
    o_ref[...] = acc[...].astype(o_ref.dtype)

    for d in range(p.nb):
        for _, m, r in p.sends(d):
            i_link(d, m, r).wait_send()
    for m in range(p.G):
        for r in range(p.RT):
            i_cross(m, r).wait_send()
    for t in range(p.R - 1):
        for kt in range(p.KT):
            for s in (1, -1):
                @pl.when(has[s] & origin_ok(t, s))
                def _():
                    a_link(t, kt, s).wait_send()


def per_device(n_row, n_col, integrals, amplitudes, int_shape, amp_shape):
    rows, i_cols = integrals.shape
    a_rows, a_cols = amplitudes.shape
    p = Plan(n_row, n_col, rows, i_cols, a_rows, a_cols)
    dma = pltpu.SemaphoreType.DMA
    return pl.pallas_call(
        functools.partial(kernel, p),
        out_shape=pltpu.VMEM((rows, a_cols), jnp.bfloat16),
        in_specs=[pl.BlockSpec(memory_space=pltpu.HBM)] * 4,
        out_specs=pl.BlockSpec(memory_space=pltpu.VMEM),
        scratch_shapes=[
            pltpu.SMEM(int_shape.shape, jnp.int32),
            pltpu.SMEM(amp_shape.shape[::-1], jnp.int32),
            pltpu.VMEM((p.G, rows, i_cols * CORES), jnp.bfloat16),
            pltpu.VMEM((p.R, a_rows, a_cols), jnp.bfloat16),
            pltpu.VMEM((rows, a_cols), jnp.float32),
            dma((4,)),
            dma((p.nb, p.G, p.RT)),
            dma((p.G, p.RT)),
            dma((p.G, CORES, p.RT)),
            dma((2, p.R, p.KT)),
            dma((p.R, p.KT)),
        ],
        compiler_params=pltpu.CompilerParams(
            collective_id=0, has_side_effects=True, vmem_limit_bytes=56 * 2**20
        ),
    )(int_shape, amp_shape.T, integrals, amplitudes)


def solution(mesh):
    in_specs = (P("row", "col"), P("row", "col"), P("row", None), P(None, "col"))
    out_specs = P("row", "col")
    body = functools.partial(per_device, mesh.shape["row"], mesh.shape["col"])
    return jax.shard_map(body, mesh=mesh, in_specs=in_specs, out_specs=out_specs, check_vma=False)
```

```python
import functools

import jax
import jax.numpy as jnp
from jax import lax
from jax.experimental import pallas as pl
from jax.experimental.pallas import tpu as pltpu
from jax.sharding import PartitionSpec as P

TILE = 256
CORES = 2
MESH = pl.DeviceIdType.MESH


class Plan:
    def __init__(self, n_row, n_col, rows, i_cols, a_rows, a_cols):
        self.R, self.C = n_row, n_col
        self.G = n_col // CORES
        self.nb = self.G.bit_length() - 1
        assert self.G == 1 << self.nb and self.G == n_row
        assert a_rows == i_cols * CORES and a_rows % TILE == 0 and rows % TILE == 0
        self.rows, self.i_cols, self.a_rows, self.a_cols = rows, i_cols, a_rows, a_cols
        self.RT, self.KT, self.QT = rows // TILE, a_rows // TILE, a_cols // TILE
        self.piece = {r: (r * self.nb) // self.RT for r in range(self.RT)}

    def dim(self, r, t):
        return (self.piece[r] + t) % self.nb

    def known(self, r, t):
        masks = [0]
        for u in range(t):
            masks += [m ^ (1 << self.dim(r, u)) for m in masks]
        return masks

    def sends(self, d):
        items = []
        for r in range(self.RT):
            for t in range(self.nb):
                if self.dim(r, t) == d:
                    items += [(t, m, r) for m in self.known(r, t)]
        return sorted(items, key=lambda i: (i[0], bin(i[1]).count("1"), i[2]))

    def events(self):
        out = []
        for d in range(self.nb):
            for n, (t, m, r) in enumerate(self.sends(d)):
                out.append(((n + 1) * self.i_cols, ("i", t, m ^ (1 << d), r)))
        for n in range((self.R - 1) * self.KT):
            out.append(((n + 1) * self.a_cols, ("a", 1 + n // self.KT, n % self.KT)))
        return [e for _, e in sorted(out, key=lambda e: e[0])]


def kernel(plan, imask_hbm, amask_hbm, i_hbm, a_hbm, o_ref, imask, amask, i_all, a_all, acc,
           local_sem, i_send, i_sib, i_recv, a_send, a_recv):
    p = plan
    z, c = lax.axis_index("row"), lax.axis_index("col")
    g, core = c // CORES, lax.rem(c, CORES)
    sibling = (z, g * CORES + 1 - core)

    def flip(value, mask):
        for b in range(p.nb):
            if mask >> b & 1:
                value = value + (1 << b) - (2 << b) * lax.rem(value // (1 << b), 2)
        return value

    def partner(d):
        return (z, flip(g, 1 << d) * CORES + core)

    has = {1: z < p.R - 1, -1: z > 0}

    bar = pltpu.get_barrier_semaphore()
    pl.semaphore_signal(bar, inc=1, device_id=sibling, device_id_type=MESH)
    for d in range(p.nb):
        pl.semaphore_signal(bar, inc=1, device_id=partner(d), device_id_type=MESH)
    for s in (1, -1):
        @pl.when(has[s])
        def _():
            pl.semaphore_signal(bar, inc=1, device_id=(z + s, c), device_id_type=MESH)
    ends = (z + p.R - 1) // p.R + (2 * p.R - 2 - z) // p.R
    pl.semaphore_wait(bar, 1 + p.nb + ends)

    def i_place(m, r, which):
        lanes = pl.ds(pl.multiple_of(which * p.i_cols, 128), p.i_cols)
        return i_all.at[flip(g, m), pl.ds(r * TILE, TILE), lanes]

    def i_source(m, r):
        return i_hbm.at[pl.ds(r * TILE, TILE)] if m == 0 else i_place(m, r, core)

    def i_link(d, m, r):
        return pltpu.make_async_remote_copy(
            i_source(m, r), i_place(m, r, core), i_send.at[d, m, r],
            i_recv.at[flip(g, m), core, r], device_id=partner(d), device_id_type=MESH)

    def i_cross(m, r):
        return pltpu.make_async_remote_copy(
            i_source(m, r), i_place(m, r, core), i_sib.at[m, r],
            i_recv.at[flip(g, m), core, r], device_id=sibling, device_id_type=MESH)

    def i_wait(m, r, which):
        pltpu.make_async_remote_copy(
            i_place(m, r, which), i_place(m, r, which), i_sib.at[m, r],
            i_recv.at[flip(g, m), which, r], device_id=sibling, device_id_type=MESH).wait_recv()

    def a_place(t, kt, s):
        return a_all.at[z - s * t, pl.ds(kt * TILE, TILE)]

    def a_link(t, kt, s):
        src = a_hbm.at[pl.ds(kt * TILE, TILE)] if t == 0 else a_place(t, kt, s)
        return pltpu.make_async_remote_copy(
            src, a_place(t, kt, s), a_send.at[(1 - s) // 2, t, kt],
            a_recv.at[z - s * t, kt], device_id=(z + s, c), device_id_type=MESH)

    def origin_ok(t, s):
        return z >= t if s == 1 else z + t <= p.R - 1

    for kt in range(p.KT):
        for s in (1, -1):
            @pl.when(has[s])
            def _():
                a_link(0, kt, s).start()
    own = [[(m, r) for _, m, r in p.sends(d) if m == 0] for d in range(p.nb)]
    for n in range(p.RT):
        for d in range(p.nb):
            i_link(d, *own[d][n]).start()
    for r in range(p.RT):
        i_cross(0, r).start()
    lanes = pl.ds(pl.multiple_of(core * p.i_cols, 128), p.i_cols)
    own_i = pltpu.make_async_copy(i_hbm, i_all.at[g, :, lanes], local_sem.at[0])
    own_a = pltpu.make_async_copy(a_hbm, a_all.at[z], local_sem.at[1])
    own_i.start()
    masks = [pltpu.make_async_copy(imask_hbm, imask, local_sem.at[2]),
             pltpu.make_async_copy(amask_hbm, amask, local_sem.at[3])]
    for copy in masks:
        copy.start()
    own_a.start()
    acc[...] = jnp.zeros_like(acc)

    def masked_right(j, kt):
        at = pl.ds(kt * TILE, TILE)
        k = j * p.KT + kt
        return [jnp.where(amask[q, k] != 0, a_all[j, at, pl.ds(q * TILE, TILE)], zero) for q in range(p.QT)]

    def masked_left(j, r, kt):
        at, cols = pl.ds(r * TILE, TILE), pl.ds(kt * TILE, TILE)
        return jnp.where(imask[r, j * p.KT + kt] != 0, i_all[j, at, cols], zero)

    zero = jnp.zeros((TILE, TILE), jnp.bfloat16)

    def product(j, kt):
        right = jnp.concatenate(masked_right(j, kt), axis=1)
        left = jnp.concatenate([masked_left(j, r, kt) for r in range(p.RT)], axis=0)
        return jnp.dot(left, right, preferred_element_type=jnp.float32)

    def multiply(j, kt):
        acc[...] += product(j, kt)

    def a_arrive(t, kt):
        for s in (1, -1):
            @pl.when(origin_ok(t, s))
            def _():
                pltpu.make_async_remote_copy(
                    a_place(t, kt, s), a_place(t, kt, s), a_send.at[0, 0, kt],
                    a_recv.at[z - s * t, kt], device_id=sibling, device_id_type=MESH).wait_recv()

                @pl.when(has[s])
                def _():
                    a_link(t, kt, s).start()

    def a_use(t, kt):
        for s in (1, -1):
            @pl.when(origin_ok(t, s))
            def _():
                if (t, kt) == (p.R - 1, p.KT - 1):
                    o_ref[...] = (acc[...] + product(z - s * t, kt)).astype(o_ref.dtype)
                else:
                    multiply(z - s * t, kt)

    events = p.events()
    last_i = max(n for n, e in enumerate(events) if e[0] == "i")
    pending = []
    for n, event in enumerate(events):
        if event[0] == "a":
            _, t, kt = event
            a_arrive(t, kt)
            if n < last_i:
                pending.append((t, kt))
            else:
                a_use(t, kt)
            continue
        _, t, m, r = event
        i_wait(m, r, core)
        for u in range(t + 1, p.nb):
            i_link(p.dim(r, u), m, r).start()
        i_cross(m, r).start()
        if n == last_i:
            own_i.wait()
            own_a.wait()
            for copy in masks:
                copy.wait()
            for m in range(p.G):
                for r in range(p.RT):
                    i_wait(m, r, 1 - core)
            for kt in range(p.KT):
                multiply(z, kt)
            for item in pending:
                a_use(*item)

    @pl.when((z > 0) & (z < p.R - 1))
    def _():
        o_ref[...] = acc[...].astype(o_ref.dtype)

    for d in range(p.nb):
        for _, m, r in p.sends(d):
            i_link(d, m, r).wait_send()
    for m in range(p.G):
        for r in range(p.RT):
            i_cross(m, r).wait_send()
    for t in range(p.R - 1):
        for kt in range(p.KT):
            for s in (1, -1):
                @pl.when(has[s] & origin_ok(t, s))
                def _():
                    a_link(t, kt, s).wait_send()


def per_device(n_row, n_col, integrals, amplitudes, int_shape, amp_shape):
    rows, i_cols = integrals.shape
    a_rows, a_cols = amplitudes.shape
    p = Plan(n_row, n_col, rows, i_cols, a_rows, a_cols)
    dma = pltpu.SemaphoreType.DMA
    return pl.pallas_call(
        functools.partial(kernel, p),
        out_shape=pltpu.VMEM((rows, a_cols), jnp.bfloat16),
        in_specs=[pl.BlockSpec(memory_space=pltpu.HBM)] * 4,
        out_specs=pl.BlockSpec(memory_space=pltpu.VMEM),
        scratch_shapes=[
            pltpu.SMEM(int_shape.shape, jnp.int32),
            pltpu.SMEM(amp_shape.shape[::-1], jnp.int32),
            pltpu.VMEM((p.G, rows, i_cols * CORES), jnp.bfloat16),
            pltpu.VMEM((p.R, a_rows, a_cols), jnp.bfloat16),
            pltpu.VMEM((rows, a_cols), jnp.float32),
            dma((4,)),
            dma((p.nb, p.G, p.RT)),
            dma((p.G, p.RT)),
            dma((p.G, CORES, p.RT)),
            dma((2, p.R, p.KT)),
            dma((p.R, p.KT)),
        ],
        compiler_params=pltpu.CompilerParams(
            collective_id=0, has_side_effects=True, vmem_limit_bytes=56 * 2**20
        ),
    )(int_shape, amp_shape.T, integrals, amplitudes)


def solution(mesh):
    in_specs = (P("row", "col"), P("row", "col"), P("row", None), P(None, "col"))
    out_specs = P("row", "col")
    body = functools.partial(per_device, mesh.shape["row"], mesh.shape["col"])
    return jax.shard_map(body, mesh=mesh, in_specs=in_specs, out_specs=out_specs, check_vma=False)
```
